128 devices in a mesh: row: 16 (over y, z), col: 8 (over x, core).
Axes of the slice: x: 4, y: 4, z: 4, core: 2. Of those that a mesh axis runs over, the one named last changes fastest.
Arguments:
- leaf_basis: bfloat16 [256, 2048, 128], P(('row', 'col')), may hold values from -6 to 6
- transfer_leaf: float32 [256, 128, 128], P(('row', 'col')), may hold values from -0.5 to 0.5
- transfer_mid: float32 [128, 128, 128], P(('row', 'col')), may hold values from -0.5 to 0.5
- transfer_top: float32 [16, 4, 128, 128], P('row'), may hold values from -0.5 to 0.5
- coupling_leaf: bfloat16 [256, 112, 128, 128], P(('row', 'col')), may hold values from -6 to 6
- coupling_mid: bfloat16 [128, 112, 128, 128], P(('row', 'col')), may hold values from -6 to 6
- partners_leaf: int32 [256, 112], P(('row', 'col')), may hold values from 0 to 255, as said below
- partners_mid: int32 [128, 112], P(('row', 'col')), may hold values from 0 to 127, as said below
- counts_leaf: int32 [256], P(('row', 'col')), may hold values from 1 to 112, as said below
- counts_mid: int32 [128], P(('row', 'col')), may hold values from 1 to 112, as said below
- ranks: int32 [4], replicated, may hold values from 64 to 128
Outputs:
- leaf_q: bfloat16 [256, 2048, 128], P(('row', 'col'))
- transfer_leaf_out: float32 [256, 128, 128], P(('row', 'col'))
- transfer_mid_out: float32 [128, 128, 128], P(('row', 'col'))
- transfer_top_out: float32 [16, 8, 64, 128], P('row', 'col')
- coupling_leaf_out: bfloat16 [256, 112, 128, 128], P(('row', 'col'))
- coupling_mid_out: bfloat16 [128, 112, 128, 128], P(('row', 'col'))
The draws below stay inside these ranges and needn't reach their ends.
Inputs may be any that keep to these rules, and one draw needn't show every extreme that they name: `partners_leaf`: A slot's partner leaf lies on a device (partner // 2) at most 6 away from the row leaf's device in the joint row-col order; distance 6 occurs. `partners_mid`: A slot's partner level-1 cluster index differs from the row cluster's by at most 6; distance 6 occurs. `counts_leaf`: some leaf has all 112 slots live. `counts_mid`: some level-1 cluster has all 112 slots live.
All inputs are finite; a program needn't handle non-finite values.
Results may differ from the reference program's by a relative error of at most 0.009.
Values sent between devices are 32-bit elements; how exact they have to be, the bound alone decides.
No kernel may reach another device: no remote copies, remote signals or barrier semaphores. Data moves between devices by JAX's collectives and lax.ppermute only.
A program may use at most 192 MiB of HBM per device.

```python
import jax
import jax.numpy as jnp
from jax import lax

K = 128
NPT = 2048
LEAF_DEV = 2
LIST = 112
SPAN = 6
BANDS = 16
COLS = 8
PAIRS = 4
MID = 128
LEAVES = 256


def partner_draw(key, clusters, per_device):
    key_offset, key_slot = jax.random.split(key)
    device = jnp.arange(clusters) // per_device
    offset = jax.random.randint(key_offset, (clusters, LIST), -SPAN, SPAN + 1)
    offset = offset.at[0, 0].set(SPAN)
    target = jnp.clip(device[:, None] + offset, 0, MID - 1)
    slot = jax.random.randint(key_slot, (clusters, LIST), 0, per_device)
    return (target * per_device + slot).astype(jnp.int32)


def count_draw(key, clusters):
    key_count, key_full = jax.random.split(key)
    counts = jax.random.randint(key_count, (clusters,), 1, LIST + 1)
    full = jax.random.randint(key_full, (), 0, clusters)
    return counts.at[full].set(LIST).astype(jnp.int32)


def draw_partners_leaf(key, part):
    return partner_draw(jax.random.fold_in(key, 31), LEAVES, LEAF_DEV)


def draw_partners_mid(key, part):
    return partner_draw(jax.random.fold_in(key, 37), MID, 1)


def draw_counts_leaf(key, part):
    return count_draw(jax.random.fold_in(key, 41), LEAVES)


def draw_counts_mid(key, part):
    return count_draw(jax.random.fold_in(key, 43), MID)


def touch_ends(array, key, low, largest):
    spot = [jax.random.randint(jax.random.fold_in(key, axis), (), 0, length) for axis, length in enumerate(array.shape)]
    widest = array.shape.index(max(array.shape))
    beside = spot[:widest] + [(spot[widest] + 1) % array.shape[widest]] + spot[widest + 1:]
    return array.at[tuple(spot)].set(low).at[tuple(beside)].set(largest)


def steps_of(key, shape, pieces, low, top_value):
    factor_of, own = 1.0, jax.random.fold_in(key, 6)
    for position, shards_of in pieces:
        steps = jnp.exp(jax.random.uniform(jax.random.fold_in(own, position), (shards_of,), jnp.float32, low / len(pieces), top_value / len(pieces)))
        factor_of = factor_of * jnp.repeat(steps, shape[position] // shards_of).reshape([-1 if axis == position else 1 for axis in range(len(shape))])
    return factor_of


def gaussian(stream_key, extent, width, most, shards=(), held_as=jnp.bfloat16):
    drawn = width * jax.random.normal(stream_key, extent, jnp.float32)
    if shards:
        drawn = drawn * steps_of(stream_key, extent, shards, -0.22, 0.18)
    return jnp.clip(drawn, -most, most).astype(held_as)


def setup_inputs(seed: int = 0) -> dict:
    streams_of = jax.random.split(jax.random.key(seed), 12)
    return {
        "leaf_basis": gaussian(streams_of[0], (LEAVES, NPT, K), 1.0, 6.0, ((0, 128),)),
        "transfer_leaf": gaussian(streams_of[1], (LEAVES, K, K), K ** -0.5, 0.5, ((0, 128),), jnp.float32),
        "transfer_mid": gaussian(streams_of[2], (MID, K, K), K ** -0.5, 0.5, ((0, 128),), jnp.float32),
        "transfer_top": gaussian(streams_of[3], (BANDS, PAIRS, K, K), K ** -0.5, 0.5, ((0, 16),), jnp.float32),
        "coupling_leaf": gaussian(streams_of[4], (LEAVES, LIST, K, K), 1.0, 6.0, ((0, 128),)),
        "coupling_mid": gaussian(streams_of[5], (MID, LIST, K, K), 1.0, 6.0, ((0, 128),)),
        "partners_leaf": draw_partners_leaf(jax.random.fold_in(streams_of[11], 71), 0),
        "partners_mid": draw_partners_mid(jax.random.fold_in(streams_of[11], 71), 0),
        "counts_leaf": draw_counts_leaf(jax.random.fold_in(streams_of[11], 71), 0),
        "counts_mid": draw_counts_mid(jax.random.fold_in(streams_of[11], 71), 0),
        "ranks": touch_ends(jax.random.randint(streams_of[10], (4,), K // 2, K + 1), jax.random.fold_in(streams_of[10], 1), K // 2, K).astype(jnp.int32),
    }


HIGHEST = lax.Precision.HIGHEST

def matmul_hi(left, right):
    return jnp.matmul(left, right, precision=HIGHEST)

def flipped(matrix):
    return jnp.swapaxes(matrix, -1, -2)

def sandwich(inner, outer):
    return matmul_hi(flipped(outer), matmul_hi(inner, outer))

def right_solve(matrix, lower_factor):
    return flipped(jax.scipy.linalg.solve_triangular(lower_factor, flipped(matrix), lower=True))

def rank_mask(count, order_k):
    return (jnp.arange(order_k) < count).astype(jnp.float32)

def transform_couplings(factors_rows, blocks, partners, counts, source, mask):
    slot_ids = jnp.arange(blocks.shape[1])

    def one_cluster(packed):
        factor, block, partner, count = packed
        picked = jnp.take(source, partner, axis=0)
        left = matmul_hi(flipped(factor)[None], block.astype(jnp.float32))
        result = matmul_hi(left, picked)
        live = (slot_ids < count).astype(jnp.float32)
        return (result * live[:, None, None] * mask[:, None] * mask[None, :]).astype(jnp.bfloat16)
    return lax.map(one_cluster, (factors_rows, blocks, partners, counts))

def reference(leaf_basis, transfer_leaf, transfer_mid, transfer_top, coupling_leaf, coupling_mid, partners_leaf, partners_mid, counts_leaf, counts_mid, ranks):
    basis = leaf_basis.astype(jnp.float32)
    gram_leaf = jnp.einsum('lpi,lpj->lij', basis, basis, precision=HIGHEST) / NPT
    factor_leaf = jnp.linalg.cholesky(gram_leaf)
    gram_mid = jnp.sum(sandwich(gram_leaf, transfer_leaf).reshape(-1, LEAF_DEV, K, K), axis=1)
    factor_mid = jnp.linalg.cholesky(gram_mid)
    gram_pair = jnp.sum(sandwich(gram_mid, transfer_mid).reshape(-1, 2, K, K), axis=1)
    factor_pair = jnp.linalg.cholesky(gram_pair)
    top_flat = transfer_top.reshape(-1, K, K)
    gram_quad = jnp.sum(sandwich(gram_pair, top_flat).reshape(-1, 2, K, K), axis=1)
    factor_quad = jnp.linalg.cholesky(gram_quad)
    masks = [rank_mask(ranks[level], K) for level in range(4)]
    leaf_q = (flipped(jax.scipy.linalg.solve_triangular(factor_leaf, flipped(basis), lower=True)) * masks[0]).astype(jnp.bfloat16)
    leaf_out = right_solve(matmul_hi(flipped(factor_leaf), transfer_leaf), jnp.repeat(factor_mid, LEAF_DEV, axis=0))
    leaf_out = leaf_out * masks[0][:, None] * masks[1][None, :]
    mid_out = right_solve(matmul_hi(flipped(factor_mid), transfer_mid), jnp.repeat(factor_pair, 2, axis=0))
    mid_out = mid_out * masks[1][:, None] * masks[2][None, :]
    top_full = right_solve(matmul_hi(flipped(factor_pair), top_flat), jnp.repeat(factor_quad, 2, axis=0))
    top_full = top_full * masks[2][:, None] * masks[3][None, :]
    top_out = top_full.reshape(BANDS, COLS, K // 2, K)
    coupling_leaf_out = transform_couplings(factor_leaf, coupling_leaf, partners_leaf, counts_leaf, factor_leaf, masks[0])
    coupling_mid_out = transform_couplings(factor_mid, coupling_mid, partners_mid, counts_mid, factor_mid, masks[1])
    return (leaf_q, leaf_out, mid_out, top_out, coupling_leaf_out, coupling_mid_out)
```

```python
import functools

import jax
import jax.numpy as jnp
from jax import lax
from jax.experimental import pallas as pl
from jax.experimental.pallas import tpu as pltpu
from jax.sharding import PartitionSpec as P

SPAN = 6
K = 128
HALF = K // 2
LIST = 112
NPT = 2048
PACK = K + HALF + 8
REACH = SPAN // 2
BLOCKS = 1 + 2 * REACH
F32 = jnp.float32
BF = jnp.bfloat16
AXES = ("row", "col")
MATS = 5
PANEL = 8
STEP = 32

VMEM = pl.BlockSpec(memory_space=pltpu.VMEM)
SMEM = pl.BlockSpec(memory_space=pltpu.SMEM)
ANY = pl.BlockSpec(memory_space=pl.ANY)


def dot_hi(left, right, cl=1, cr=0):
    return lax.dot_general(
        left, right, (((cl,), (cr,)), ((), ())),
        precision=lax.Precision.HIGHEST, preferred_element_type=F32,
    )


def dot_bf(left, right, cl=1, cr=0):
    return lax.dot_general(
        left, right, (((cl,), (cr,)), ((), ())), preferred_element_type=F32
    )


def sandwich(inner, outer):
    return dot_hi(outer, dot_hi(inner, outer), 0, 0)


def iotas(rows, cols):
    return (
        lax.broadcasted_iota(jnp.int32, (rows, cols), 0),
        lax.broadcasted_iota(jnp.int32, (rows, cols), 1),
    )


def split2(x):
    high = x.astype(BF)
    return high, (x - high.astype(F32)).astype(BF)


def split3(x):
    high = x.astype(BF)
    rest = x - high.astype(F32)
    mid = rest.astype(BF)
    return high, mid, (rest - mid.astype(F32)).astype(BF)


def grams_kernel(basis, tleaf, tmid, leaf_out, mid_out, pair_out):
    total = None
    for t in range(2):
        points = basis[t]
        gram = dot_bf(points, points, 0, 0) / NPT
        leaf_out[t] = gram
        term = sandwich(gram, tleaf[t])
        total = term if total is None else total + term
    mid_out[0] = total
    pair_out[0] = sandwich(total, tmid[0])


def quad_kernel(where, term, other, top, pair_out, quad_out):
    pair = term[0] + other[0]
    pair_out[0] = pair
    quad_out[0] = sandwich(pair, top[0, where[0]])


def broadcast_lane(row, lane):
    return jnp.broadcast_to(row[:, lane : lane + 1], row.shape)


def eliminate(grows, erows, base):
    count = len(grows)
    grows, erows = list(grows), list(erows)
    for k0 in range(0, count, PANEL):
        g = grows[k0 : k0 + PANEL]
        e = erows[k0 : k0 + PANEL]
        v = {(m, j): broadcast_lane(g[m], base + k0 + j) for m in range(PANEL) for j in range(m + 1)}
        for j in range(PANEL):
            scale = lax.rsqrt(v[j, j])
            g[j] = g[j] * scale
            e[j] = e[j] * scale
            low = {m: v[m, j] * scale for m in range(j + 1, PANEL)}
            for m in range(j + 1, PANEL):
                for i in range(j + 1, m + 1):
                    v[m, i] = v[m, i] - low[m] * low[i]
                g[m] = g[m] - low[m] * g[j]
                e[m] = e[m] - low[m] * e[j]
        grows[k0 : k0 + PANEL] = g
        erows[k0 : k0 + PANEL] = e
        for m in range(k0 + PANEL, count):
            a, x = grows[m], erows[m]
            for j in range(PANEL):
                c = broadcast_lane(g[j], base + m)
                a = a - c * g[j]
                x = x - c * e[j]
            grows[m], erows[m] = a, x
    return grows, erows


def factor_kernel(gleaf, gmid, gpair, term, other, upper_out, inverse_out, pack_out, wg, we):
    io, jo = iotas(K, K)
    eye = io == jo
    grams = [gleaf[0], gleaf[1], gmid[0], gpair[0], term[0] + other[0]]
    for s in range(MATS):
        wg[pl.ds(s, K, stride=8), :] = grams[s]
        we[pl.ds(s, K, stride=8), :] = eye.astype(F32)
    for s in range(MATS, 8):
        wg[pl.ds(s, K, stride=8), :] = eye.astype(F32)
        we[pl.ds(s, K, stride=8), :] = eye.astype(F32)
    for b in range(0, K, STEP):
        g = [wg[8 * m : 8 * m + 8, :] for m in range(b, b + STEP)]
        e = [we[8 * m : 8 * m + 8, :] for m in range(b, b + STEP)]
        g, e = eliminate(g, e, b)
        for i in range(STEP):
            wg[8 * (b + i) : 8 * (b + i) + 8, :] = g[i]
            we[8 * (b + i) : 8 * (b + i) + 8, :] = e[i]
        rest = K - b - STEP
        if rest:
            for s in range(MATS):
                h, m, l = split3(wg[pl.ds(8 * b + s, STEP, stride=8), :])
                xh, xm, xl = split3(we[pl.ds(8 * b + s, STEP, stride=8), :])
                left = jnp.concatenate([h, h, m, h, l, m], 0)
                right = jnp.concatenate(
                    [
                        jnp.concatenate([h, m, h, l, h, m], 0),
                        jnp.concatenate([xh, xm, xh, xl, xh, xm], 0),
                    ],
                    1,
                )
                update = dot_bf(left, right, 0, 0)
                rows = pl.ds(8 * (b + STEP) + s, rest, stride=8)
                wg[rows, :] = wg[rows, :] - update[b + STEP :, :K]
                we[rows, :] = we[rows, :] - update[b + STEP :, K:]
    upper = [jnp.where(jo >= io, wg[pl.ds(s, K, stride=8), :], 0.0) for s in range(MATS)]
    for s in range(MATS):
        upper_out[s] = upper[s]
        inverse_out[s] = we[pl.ds(s, K, stride=8), :]
    pack_out[:K, :] = jnp.where(jo >= io, upper[0], upper[1].T)
    ih, jh = iotas(HALF, K)
    corner = upper[2][HALF:, HALF:].T
    corner = jnp.concatenate([corner, jnp.zeros((HALF, HALF), F32)], 1)
    pack_out[K : K + HALF, :] = jnp.where(jh >= ih, upper[2][:HALF], corner)
    for row, s in enumerate((1, 2)):
        pack_out[K + HALF + row : K + HALF + row + 1, :] = jnp.sum(
            jnp.where(eye, upper[s], 0.0), axis=0, keepdims=True
        )
    pack_out[K + HALF + 2 :, :] = jnp.zeros((6, K), F32)


def small_kernel(where, ranks, upper, inverse, tleaf, tmid, top, basis, q_out, lout, mout, tout):
    io, jo = iotas(K, K)
    row_mask = [(io < ranks[l]).astype(F32) for l in range(4)]
    col_mask = [(jo < ranks[l]).astype(F32) for l in range(4)]
    for t in range(2):
        high, low = split2(inverse[t] * row_mask[0])
        pair = jnp.concatenate([high, low], 1)
        for c in range(0, NPT, 512):
            points = basis[t, c : c + 512]
            both = jnp.concatenate([points, points], 1)
            q_out[t, c : c + 512] = dot_bf(both, pair, 1, 1).astype(BF)
        out = dot_hi(dot_hi(upper[t], tleaf[t]), inverse[2], 1, 1)
        lout[t] = out * row_mask[0] * col_mask[1]
    mout[0] = dot_hi(dot_hi(upper[2], tmid[0]), inverse[3], 1, 1) * row_mask[1] * col_mask[2]
    start = where[1] * HALF
    half = upper[3, pl.ds(pl.multiple_of(start, HALF), HALF), :]
    out = dot_hi(dot_hi(half, top[0, where[0]]), inverse[4], 1, 1)
    ih, _ = iotas(HALF, K)
    keep = (ih + start < ranks[2]).astype(F32)
    tout[0, 0] = out * keep * col_mask[3][:HALF]


def unpack(pack, base, masks, store, index):
    io, jo = iotas(K, K)
    p0 = pack[base : base + K, :]
    pm = pack[base + K : base + K + HALF, :]
    d1 = pack[base + K + HALF : base + K + HALF + 1, :]
    dm = pack[base + K + HALF + 1 : base + K + HALF + 2, :]
    first = jnp.where(jo >= io, p0, 0.0).T
    store[index] = (first * masks[0]).astype(BF)
    second = jnp.where(jo < io, p0, jnp.where(jo == io, d1, 0.0))
    store[index + 1] = (second * masks[0]).astype(BF)
    ih, jh = iotas(HALF, K)
    top = jnp.where(jh >= ih, pm, 0.0).T
    ic, jc = iotas(HALF, HALF)
    corner = jnp.where(jc < ic, pm[:, :HALF], jnp.where(jc == ic, dm[:, HALF:], 0.0))
    corner = jnp.concatenate([jnp.zeros((HALF, HALF), F32), corner], 0)
    third = jnp.concatenate([top, corner], 1)
    store[index + 2] = (third * masks[1]).astype(BF)


GROUP = 56


def coupling_kernel(
    me, ranks, counts_leaf, counts_mid, partners_leaf, partners_mid, upper,
    own, a1, a2, a3, b1, b2, b3, cleaf, cmid, out_leaf, out_mid,
    store, table, rows, zbuf, sems,
):
    io, jo = iotas(K, K)
    masks = [(jo < ranks[l]).astype(F32) for l in range(2)]
    keeps = [(io < ranks[l]).astype(F32) for l in range(2)]
    for block, pack in enumerate((own, a1, a2, a3, b1, b2, b3)):
        for h in range(2):
            unpack(pack, h * PACK, masks, store, (block * 2 + h) * 3)
    for s in range(3):
        high, low = split2(upper[s] * keeps[0 if s < 2 else 1])
        rows[s] = jnp.concatenate([high, low], 1)
    device = me[0]
    parity = device & 1
    sign = 1 - 2 * parity
    for d in range(-SPAN, SPAN + 1):
        other = device + d
        delta = (other >> 1) - (device >> 1)
        apart = jnp.abs(delta)
        mine = delta * sign < 0
        block = jnp.where(mine, apart, jnp.where(delta == 0, 0, REACH + apart))
        first = jnp.where(jnp.logical_or(mine, delta == 0), parity, 1 - parity)
        table[d + SPAN] = (block * 2 + ((other & 1) ^ first)) * 3

    per = LIST // GROUP
    copies = []
    for group in range(3 * per):
        s, j0 = group // per, (group % per) * GROUP
        count = counts_leaf[s] if s < 2 else counts_mid[0]
        slot = group % 2
        if group >= 2:
            copies[group - 2].wait()
        for p in range(0, GROUP, 2):
            j = j0 + p
            if s < 2:
                blocks = [cleaf[s, j], cleaf[s, j + 1]]
                mates = [partners_leaf[s, j + q] for q in range(2)]
                index = [table[(m >> 1) - device + SPAN] + (m & 1) for m in mates]
            else:
                blocks = [cmid[0, j], cmid[0, j + 1]]
                mates = [partners_mid[0, j + q] for q in range(2)]
                index = [table[m - device + SPAN] + 2 for m in mates]
            both = jnp.concatenate(blocks, 1)
            left = dot_bf(rows[s], jnp.concatenate([both, both], 0)).astype(BF)
            for q in range(2):
                z = dot_bf(left[:, q * K : q * K + K], store[index[q]])
                live = (j + q < count).astype(F32)
                zbuf[slot, p + q] = (z * live).astype(BF)
        target = out_leaf.at[s, pl.ds(j0, GROUP)] if s < 2 else out_mid.at[0, pl.ds(j0, GROUP)]
        copy = pltpu.make_async_copy(zbuf.at[slot], target, sems.at[slot])
        copy.start()
        copies.append(copy)
    copies[-2].wait()
    copies[-1].wait()


def shaped(*shape, dtype=F32):
    return jax.ShapeDtypeStruct(shape, dtype)


def swap_core(value, bit):
    size = lax.axis_size("col")
    return lax.ppermute(value, "col", [(i, i ^ (1 << bit)) for i in range(size)])


def from_chip(value, apart):
    total = lax.axis_size(AXES)
    route = []
    for source in range(total):
        target = source + 2 * apart if source % 2 == 0 else source - 2 * apart
        if 0 <= target < total:
            route.append((source, target))
    return lax.ppermute(value, AXES, route)


def params(mib):
    return pltpu.CompilerParams(vmem_limit_bytes=mib << 20)


def on_device(
    leaf_basis, transfer_leaf, transfer_mid, transfer_top, coupling_leaf, coupling_mid,
    partners_leaf, partners_mid, counts_leaf, counts_mid, ranks,
):
    col = lax.axis_index("col")
    me = lax.axis_index(AXES).reshape(1)
    where = jnp.stack([col // 2, col % 2])
    gleaf, gmid, term_pair = pl.pallas_call(
        grams_kernel, name="grams",
        out_shape=[shaped(2, K, K), shaped(1, K, K), shaped(1, K, K)],
        in_specs=[VMEM] * 3, out_specs=[VMEM] * 3, compiler_params=params(8),
    )(leaf_basis, transfer_leaf, transfer_mid)
    gpair, term_quad = pl.pallas_call(
        quad_kernel, name="quad",
        out_shape=[shaped(1, K, K), shaped(1, K, K)],
        in_specs=[SMEM] + [VMEM] * 3, out_specs=[VMEM] * 2, compiler_params=params(8),
    )(where, term_pair, swap_core(term_pair, 0), transfer_top)
    upper, inverse, pack = pl.pallas_call(
        factor_kernel, name="factor",
        out_shape=[shaped(MATS, K, K), shaped(MATS, K, K), shaped(PACK, K)],
        in_specs=[VMEM] * 5, out_specs=[VMEM] * 3,
        scratch_shapes=[pltpu.VMEM((8 * K, K), F32)] * 2, compiler_params=params(12),
    )(gleaf, gmid, gpair, term_quad, swap_core(term_quad, 1))
    own = jnp.concatenate([pack, swap_core(pack, 0)], 0)
    near = [from_chip(own, d) for d in range(1, REACH + 1)]
    far = [swap_core(block, 0) for block in near]
    leaf_q, leaf_out, mid_out, top_out = pl.pallas_call(
        small_kernel, name="small",
        out_shape=[
            shaped(2, NPT, K, dtype=BF), shaped(2, K, K), shaped(1, K, K), shaped(1, 1, HALF, K),
        ],
        in_specs=[SMEM] * 2 + [VMEM] * 6, out_specs=[VMEM] * 4, compiler_params=params(12),
    )(where, ranks, upper, inverse, transfer_leaf, transfer_mid, transfer_top, leaf_basis)
    out_leaf, out_mid = pl.pallas_call(
        coupling_kernel, name="coupling",
        out_shape=[shaped(2, LIST, K, K, dtype=BF), shaped(1, LIST, K, K, dtype=BF)],
        in_specs=[SMEM] * 6 + [VMEM] * 10, out_specs=[ANY] * 2,
        scratch_shapes=[
            pltpu.VMEM((BLOCKS * 6, K, K), BF), pltpu.SMEM((16,), jnp.int32),
            pltpu.VMEM((3, K, 2 * K), BF), pltpu.VMEM((2, GROUP, K, K), BF),
            pltpu.SemaphoreType.DMA((2,)),
        ],
        compiler_params=params(24),
    )(me, ranks, counts_leaf, counts_mid, partners_leaf, partners_mid, upper, own, *near, *far,
      coupling_leaf, coupling_mid)
    return (leaf_q, leaf_out, mid_out, top_out, out_leaf, out_mid)


def solution(mesh):
    both = ("row", "col")
    in_specs = (
        P(both, None, None),
        P(both, None, None),
        P(both, None, None),
        P("row", None, None, None),
        P(both, None, None, None),
        P(both, None, None, None),
        P(both, None),
        P(both, None),
        P(both),
        P(both),
        P(),
    )
    out_specs = (
        P(both, None, None),
        P(both, None, None),
        P(both, None, None),
        P("row", "col", None, None),
        P(both, None, None, None),
        P(both, None, None, None),
    )
    return jax.shard_map(
        on_device, mesh=mesh, in_specs=in_specs, out_specs=out_specs, check_vma=False
    )
```
